32 devices in a mesh: rows: 8 (over z, y), cols: 4 (over x, core).
Axes of the slice: x: 2, y: 2, z: 4, core: 2. Of those that a mesh axis runs over, the one named last changes fastest.
Arguments:
- tiles: bfloat16 [2, 8, 4, 128, 128, 128], P(None, 'rows', 'cols'), may hold values from -0.15625 to 0.15625
- tile_scales: float32 [2, 8, 4, 128], P(None, 'rows', 'cols'), may hold values from 0.5 to 4
- tile_rows: int32 [2, 8, 4, 128], P(None, 'rows', 'cols'), may hold values from 0 to 7
- tile_cols: int32 [2, 8, 4, 128], P(None, 'rows', 'cols'), may hold values from 0 to 1023
- tile_counts: int32 [2, 8, 4], P(None, 'rows', 'cols'), may hold values from 32 to 128, as said below
- labels: int32 [2, 8192], P(None, 'rows'), may hold values from 0 to 31
- learning_rate: float32 [2], replicated, may hold values from 4 to 16
- weights: float32 [32, 524288], P(None, ('cols', 'rows')), may hold values from -6 to 6
Outputs:
- trained: float32 [32, 524288], P(None, ('cols', 'rows'))
- losses: float32 [2, 8192], P(None, ('rows', 'cols'))
The draws below stay inside these ranges and needn't reach their ends.
Inputs may be any that keep to these rules, and one draw needn't show every extreme that they name: Only the first tile_counts[s, r, c] slots of a block are live; in every step some block has all 128 slots live.
All inputs are finite; a program needn't handle non-finite values.
Results may differ from the reference program's by a relative error of at most 0.0021.
Values may be sent and summed in bfloat16 or wider, within the bound.
A program may use at most 128 MiB of HBM per device.

```python
import math
import jax
import jax.numpy as jnp
from jax import lax

CLASS_COUNT = 32
F = 524288
BLK = 128
STEPS = 2
STEP_SAMPLES = 1024
TILES = 128
SAMPLES = 8192
FB_DEV = 1024
RB_DEV = 8
N_ROWS = 8
N_COLS = 4


def draw_tile_counts(key, part):
    shifts = jax.random.randint(key, (STEPS, N_ROWS * N_COLS), 0, 3)
    counts = TILES // jnp.left_shift(jnp.ones_like(shifts), shifts)
    fullest = jax.random.randint(jax.random.fold_in(key, 7), (STEPS, 1), 0, N_ROWS * N_COLS)
    places = jnp.arange(N_ROWS * N_COLS, dtype=jnp.int32)[None, :]
    counts = jnp.where(places == fullest, TILES, counts)
    return counts.reshape(STEPS, N_ROWS, N_COLS).astype(jnp.int32)


def set_ends(entries, rng, smallest, top_value):
    place = [jax.random.randint(jax.random.fold_in(rng, axis), (), 0, length) for axis, length in enumerate(entries.shape)]
    longest = entries.shape.index(max(entries.shape))
    next_to = place[:longest] + [(place[longest] + 1) % entries.shape[longest]] + place[longest + 1:]
    return entries.at[tuple(place)].set(smallest).at[tuple(next_to)].set(top_value)


def levels(rng, shape, pieces, low, top_value):
    gain = 1.0
    for position, shards_of in pieces:
        heights = jax.random.uniform(jax.random.fold_in(jax.random.fold_in(rng, 6), position), (shards_of,), jnp.float32, low / len(pieces), top_value / len(pieces))
        gain = gain * jnp.repeat(jnp.exp(heights), shape[position] // shards_of).reshape((-1,) + (1,) * (len(shape) - 1 - position))
    return gain


def scatter_about(own_key, extent, spread, bound, shards=(), kind=jnp.bfloat16):
    array = jax.random.normal(own_key, extent, jnp.float32) * spread
    if len(shards) > 0:
        array = levels(own_key, extent, shards, -0.22, 0.18) * array
    return jnp.clip(array, min=-bound, max=bound).astype(kind)


def setup_inputs(seed: int = 0) -> dict:
    key_of = jax.random.split(jax.random.key(seed), 9)
    tiles = scatter_about(key_of[0], (STEPS, N_ROWS, N_COLS, TILES, BLK, BLK), ((BLK * BLK * TILES * N_COLS // STEP_SAMPLES) ** -0.5), 0.15625, ((1, 8), (2, 4)))
    tile_scales = jnp.clip(jnp.exp(math.log(4.0) - 2.0794415 * jax.random.uniform(key_of[1], (STEPS, N_ROWS, N_COLS, TILES), jnp.float32) ** levels(key_of[1], (STEPS, N_ROWS, N_COLS, TILES), ((1, 8), (2, 4)), -0.2, 0.2)), 0.5, 4.0)
    tile_rows = set_ends(jax.random.randint(key_of[2], (STEPS, N_ROWS, N_COLS, TILES), 0, RB_DEV), jax.random.fold_in(key_of[2], 1), 0, RB_DEV - 1).astype(jnp.int32)
    tile_cols = set_ends(jax.random.randint(key_of[3], (STEPS, N_ROWS, N_COLS, TILES), 0, FB_DEV), jax.random.fold_in(key_of[3], 1), 0, FB_DEV - 1).astype(jnp.int32)
    tile_counts = draw_tile_counts(jax.random.fold_in(key_of[8], 71), 0)
    labels = set_ends(jax.random.randint(key_of[5], (STEPS, SAMPLES), 0, CLASS_COUNT), jax.random.fold_in(key_of[5], 1), 0, CLASS_COUNT - 1).astype(jnp.int32)
    learning_rate = jnp.clip(jnp.exp(jax.random.uniform(key_of[6], (STEPS,), jnp.float32, math.log(4.0), math.log(16.0))), 4.0, 16.0)
    weights = scatter_about(key_of[7], (CLASS_COUNT, F), 1.5, 6.0, ((1, 32),), jnp.float32)
    return dict(tiles=tiles, tile_scales=tile_scales, tile_rows=tile_rows, tile_cols=tile_cols, tile_counts=tile_counts, labels=labels, learning_rate=learning_rate, weights=weights)


def reference(tiles, tile_scales, tile_rows, tile_cols, tile_counts, labels, learning_rate, weights):
    col_blocks = F // (BLK * N_COLS)
    row_blocks = STEP_SAMPLES // BLK
    slot_ids = jnp.arange(TILES, dtype=jnp.int32)
    block_ids = jnp.arange(row_blocks, dtype=jnp.int32)
    class_ids = jnp.arange(CLASS_COUNT, dtype=jnp.int32)
    col_offsets = (jnp.arange(N_COLS, dtype=jnp.int32) * col_blocks)[:, None]
    current = weights
    losses = []
    for step_index in range(STEPS):
        wide_blocks = current.astype(jnp.bfloat16).reshape(CLASS_COUNT, F // BLK, BLK)

        def one_row(grad_sum, row_index):
            tile_entries = tiles[step_index][row_index].reshape(N_COLS * TILES, BLK, BLK).astype(jnp.float32)
            is_live = slot_ids[None, :] < tile_counts[step_index][row_index][:, None]
            factor = jnp.where(is_live, tile_scales[step_index][row_index], 0.0).reshape(-1)
            col_ids = (tile_cols[step_index][row_index] + col_offsets).reshape(-1).astype(jnp.int32)
            row_ids = tile_rows[step_index][row_index].reshape(-1).astype(jnp.int32)
            selected_entries = jnp.take(wide_blocks, col_ids, axis=1).astype(jnp.float32)
            weighted_products = jnp.einsum("zei,eui->ezu", selected_entries, tile_entries, precision=lax.Precision.HIGHEST)
            row_indicator = (row_ids[:, None] == block_ids[None, :]).astype(jnp.float32) * factor[:, None]
            class_scores = jnp.einsum("iu,idq->duq", row_indicator, weighted_products, precision=lax.Precision.HIGHEST).reshape(CLASS_COUNT, STEP_SAMPLES)
            step_labels = lax.dynamic_slice_in_dim(labels[step_index], (row_index * STEP_SAMPLES).astype(jnp.int32), STEP_SAMPLES)
            exp_logits = jnp.exp(class_scores)
            denominator = jnp.sum(exp_logits, axis=0)
            onehot = (class_ids[:, None] == step_labels[None, :]).astype(jnp.float32)
            sample_loss = jnp.log(denominator) - jnp.sum(onehot * class_scores, axis=0)
            residual = (exp_logits / denominator - onehot).astype(jnp.bfloat16)
            picked_rows = jnp.take(residual.reshape(CLASS_COUNT, row_blocks, BLK), row_ids, axis=1).astype(jnp.float32)
            grad_blocks = jnp.einsum("cts,tsf->ctf", picked_rows, tile_entries, precision=lax.Precision.HIGHEST) * factor[None, :, None]
            grad_sum = grad_sum.at[:, col_ids, :].add(grad_blocks)
            return grad_sum, sample_loss

        grad_sum, row_losses = lax.scan(one_row, jnp.zeros((CLASS_COUNT, F // BLK, BLK), jnp.float32), jnp.arange(N_ROWS, dtype=jnp.int32))
        current = current - learning_rate[step_index] * grad_sum.reshape(CLASS_COUNT, F)
        losses.append(row_losses.reshape(-1))
    return current, jnp.stack(losses)
```

```python
import functools
import math
import jax
import jax.numpy as jnp
from jax import lax
from jax.experimental import pallas as pl
from jax.experimental.pallas import tpu as pltpu
from jax.sharding import PartitionSpec as P

MESH = pl.DeviceIdType.MESH
VMEM_LIMIT = 48 * 1024 * 1024


def classify(class_scores, step_labels):
    exp_logits = jnp.exp(class_scores)
    denominator = jnp.sum(exp_logits, axis=0)
    class_ids = jnp.arange(class_scores.shape[0], dtype=jnp.int32)
    onehot = (class_ids[:, None] == step_labels[None, :]).astype(jnp.float32)
    sample_loss = jnp.log(denominator) - jnp.sum(onehot * class_scores, axis=0)
    residual = (exp_logits / denominator - onehot).astype(jnp.bfloat16)
    return (sample_loss, residual)


def dense_program(
    tiles, tile_scales, tile_rows, tile_cols, tile_counts, labels, learning_rate, weights
):
    classes = weights.shape[0]
    tile_size = tiles.shape[-1]
    slot_count = tiles.shape[3]
    step_count = tiles.shape[0]
    sample_count = labels.shape[1]
    row_blocks = sample_count // tile_size
    owned_size = sample_count // lax.axis_size("cols")
    owned_start = lax.axis_index("cols") * owned_size
    slot_ids = jnp.arange(slot_count, dtype=jnp.int32)
    block_ids = jnp.arange(row_blocks, dtype=jnp.int32)
    current = weights
    step_losses = []
    for step_index in range(step_count):
        wide_bf = lax.all_gather(current.astype(jnp.bfloat16), "rows", axis=1, tiled=True)
        wide_blocks = wide_bf.reshape(classes, -1, tile_size)
        tile_entries = tiles[step_index, 0, 0]
        row_ids = tile_rows[step_index, 0, 0]
        col_ids = tile_cols[step_index, 0, 0]
        factor = jnp.where(
            slot_ids < tile_counts[step_index, 0, 0], tile_scales[step_index, 0, 0], 0.0
        )
        selected_weights = jnp.take(wide_blocks, col_ids, axis=1)
        weighted_products = jnp.einsum(
            "zei,eui->ezu", selected_weights, tile_entries, preferred_element_type=jnp.float32
        )
        row_indicator = (row_ids[:, None] == block_ids[None, :]).astype(jnp.float32) * factor[
            :, None
        ]
        partial_value = jnp.einsum(
            "iu,idq->duq", row_indicator, weighted_products, precision=lax.Precision.HIGHEST
        ).reshape(classes, sample_count)
        step_labels = labels[step_index]
        owned_logits = lax.psum_scatter(partial_value, "cols", scatter_dimension=1, tiled=True)
        owned_labels = lax.dynamic_slice_in_dim(step_labels, owned_start, owned_size)
        owned_loss, owned_residual = classify(owned_logits, owned_labels)
        residual = lax.all_gather(owned_residual, "cols", axis=1, tiled=True)
        step_losses.append(owned_loss)
        picked_rows = jnp.take(residual.reshape(classes, row_blocks, tile_size), row_ids, axis=1)
        grad_blocks = (
            jnp.einsum(
                "cts,tsf->ctf", picked_rows, tile_entries, preferred_element_type=jnp.float32
            )
            * factor[None, :, None]
        )
        local_grad = (
            jnp.zeros((classes, wide_blocks.shape[1], tile_size), jnp.float32)
            .at[:, col_ids, :]
            .add(grad_blocks)
            .reshape(classes, -1)
        )
        step_rate = learning_rate[step_index]
        grad_share = lax.psum_scatter(local_grad, "rows", scatter_dimension=1, tiled=True)
        current = current - step_rate * grad_share
    return (current, jnp.stack(step_losses))


def lanes(block, size):
    return pl.ds(pl.multiple_of(block * size, size), size)


def pack_body(size, next_ref, weights_ref, send_ref):
    @pl.loop(0, send_ref.shape[0] // 8)
    def _(group):
        for lane in range(8):
            entry = group * 8 + lane
            send_ref[entry] = weights_ref[:, lanes(next_ref[entry], size)].astype(jnp.bfloat16)


def apply_body(size, here_ref, rate_ref, weights_ref, grads_ref, out_ref):
    out_ref[...] = weights_ref[...]
    rate = rate_ref[0]

    @pl.loop(0, grads_ref.shape[0] // 8)
    def _(group):
        for lane in range(8):
            entry = group * 8 + lane
            where = lanes(here_ref[entry], size)
            out_ref[:, where] -= rate * grads_ref[entry].astype(jnp.float32)


def pack_kernel(size, next_ref, weights_ref, send_ref):
    pack_body(size, next_ref, weights_ref, send_ref)


def apply_kernel(size, here_ref, rate_ref, weights_ref, grads_ref, out_ref):
    apply_body(size, here_ref, rate_ref, weights_ref, grads_ref, out_ref)


def apply_pack_kernel(
    size, here_ref, next_ref, rate_ref, weights_ref, grads_ref, out_ref, send_ref
):
    apply_body(size, here_ref, rate_ref, weights_ref, grads_ref, out_ref)
    pack_body(size, next_ref, out_ref, send_ref)


def exchange_kernel(axis, count, send_ref, recv_ref, send_sems, recv_sems, own_sem):
    me = lax.axis_index(axis)
    barrier = pltpu.get_barrier_semaphore()
    for shift in range(1, count):
        peer = lax.rem(me + shift, count)
        pl.semaphore_signal(barrier, inc=1, device_id={axis: peer}, device_id_type=MESH)
    own = pltpu.make_async_copy(send_ref.at[me], recv_ref.at[me], own_sem)
    own.start()
    pl.semaphore_wait(barrier, count - 1)
    copies = []
    for shift in range(1, count):
        peer = lax.rem(me + shift, count)
        copy = pltpu.make_async_remote_copy(
            src_ref=send_ref.at[peer],
            dst_ref=recv_ref.at[me],
            send_sem=send_sems.at[shift],
            recv_sem=recv_sems.at[shift],
            device_id={axis: peer},
            device_id_type=MESH,
        )
        copy.start()
        copies.append(copy)
    own.wait()
    for copy in copies:
        copy.wait()


def exchange(send, axis, count, collective_id):
    return pl.pallas_call(
        functools.partial(exchange_kernel, axis, count),
        out_shape=jax.ShapeDtypeStruct(send.shape, send.dtype),
        in_specs=[pl.BlockSpec(memory_space=pl.ANY)],
        out_specs=pl.BlockSpec(memory_space=pl.ANY),
        scratch_shapes=[
            pltpu.SemaphoreType.DMA((count,)),
            pltpu.SemaphoreType.DMA((count,)),
            pltpu.SemaphoreType.DMA,
        ],
        compiler_params=pltpu.CompilerParams(collective_id=collective_id, has_side_effects=True),
        name="exchange",
    )(send)


def scores_kernel(group, size, place_ref, row_ref, factor_ref, recv_ref, tiles_ref, out_ref):
    first = pl.program_id(0) * group

    @pl.when(first == 0)
    def _():
        out_ref[...] = jnp.zeros_like(out_ref)

    products = []
    for slot in range(group):
        product = lax.dot_general(
            recv_ref[place_ref[first + slot]],
            tiles_ref[0, 0, 0, slot],
            (((1,), (1,)), ((), ())),
            preferred_element_type=jnp.float32,
        )
        products.append(product * factor_ref[first + slot])
    for slot in range(group):
        out_ref[:, lanes(row_ref[first + slot], size)] += products[slot]


def classify_kernel(
    axis, count, part_ref, labels_ref, residual_ref, loss_ref, held, send_sems, recv_sems
):
    me = lax.axis_index(axis)
    barrier = pltpu.get_barrier_semaphore()
    for shift in range(1, count):
        peer = lax.rem(me + shift, count)
        pl.semaphore_signal(barrier, inc=1, device_id={axis: peer}, device_id_type=MESH)
    pl.semaphore_wait(barrier, count - 1)
    copies = []
    for shift in range(1, count):
        peer = lax.rem(me + shift, count)
        copy = pltpu.make_async_remote_copy(
            src_ref=part_ref,
            dst_ref=held.at[shift],
            send_sem=send_sems.at[shift],
            recv_sem=recv_sems.at[shift],
            device_id={axis: peer},
            device_id_type=MESH,
        )
        copy.start()
        copies.append(copy)
    scores = part_ref[...]
    for shift, copy in enumerate(copies):
        copy.wait()
        scores = scores + held[shift + 1]
    exp_scores = jnp.exp(scores)
    total = jnp.sum(exp_scores, axis=0, keepdims=True)
    class_ids = lax.broadcasted_iota(jnp.int32, scores.shape, 0)
    onehot = (class_ids == labels_ref[...]).astype(jnp.float32)
    loss_ref[...] = jnp.log(total) - jnp.sum(onehot * scores, axis=0, keepdims=True)
    residual_ref[...] = (exp_scores / total - onehot).astype(jnp.bfloat16)


def grads_kernel(
    group, size, place_ref, row_ref, factor_ref, residual_ref, tiles_ref, out_ref, total
):
    first = pl.program_id(0) * group

    @pl.when(first == 0)
    def _():
        total[...] = jnp.zeros_like(total)

    products = []
    for slot in range(group):
        product = jnp.dot(
            residual_ref[:, lanes(row_ref[first + slot], size)],
            tiles_ref[0, 0, 0, slot],
            preferred_element_type=jnp.float32,
        )
        products.append(product * factor_ref[first + slot])
    for slot in range(group):
        total[place_ref[first + slot]] += products[slot]

    @pl.when(pl.program_id(0) == pl.num_programs(0) - 1)
    def _():
        out_ref[...] = total[...].astype(jnp.bfloat16)


VM = pl.BlockSpec(memory_space=pltpu.VMEM)
SM = pl.BlockSpec(memory_space=pltpu.SMEM)
LOCAL = pltpu.CompilerParams(vmem_limit_bytes=VMEM_LIMIT)


def slot_call(kernel, step, tiles, scalars, operand, out_shape, scratch, name):
    group = 16
    size = tiles.shape[-1]
    zeros = lambda rank: (lambda i, *_: (0,) * rank)
    return pl.pallas_call(
        functools.partial(kernel, group, size),
        grid_spec=pltpu.PrefetchScalarGridSpec(
            num_scalar_prefetch=3,
            grid=(tiles.shape[3] // group,),
            in_specs=[
                pl.BlockSpec(operand.shape, zeros(operand.ndim)),
                pl.BlockSpec((1, 1, 1, group, size, size), lambda i, *_: (step, 0, 0, i, 0, 0)),
            ],
            out_specs=pl.BlockSpec(out_shape.shape, zeros(len(out_shape.shape))),
            scratch_shapes=scratch,
        ),
        out_shape=out_shape,
        compiler_params=LOCAL,
        name=name,
    )(*scalars, operand, tiles)


def sparse_program(
    capacity, places, requests,
    tiles, tile_scales, tile_rows, tile_cols, tile_counts, labels, learning_rate, weights
):
    classes = weights.shape[0]
    size = tiles.shape[-1]
    steps, slots = tiles.shape[0], tiles.shape[3]
    n_rows, n_cols = lax.axis_size("rows"), lax.axis_size("cols")
    samples = labels.shape[1]
    entries = n_rows * capacity
    packed = jax.ShapeDtypeStruct((entries, classes, size), jnp.bfloat16)
    slot_ids = jnp.arange(slots, dtype=jnp.int32)
    owned = samples // n_cols
    trade = lambda x: exchange(
        x.reshape(n_rows, capacity, classes, size), "rows", n_rows, 0
    ).reshape(packed.shape)

    current = weights
    send = pl.pallas_call(
        functools.partial(pack_kernel, size),
        out_shape=packed, in_specs=[SM, VM], out_specs=VM, compiler_params=LOCAL, name="pack",
    )(requests[0], current)
    losses = []
    for step in range(steps):
        factor = jnp.where(slot_ids < tile_counts[step, 0, 0], tile_scales[step, 0, 0], 0.0)
        scalars = (places[step], tile_rows[step, 0, 0], factor)
        part = slot_call(
            scores_kernel, step, tiles, scalars, trade(send),
            jax.ShapeDtypeStruct((classes, samples), jnp.float32), [], "scores",
        )
        residual, loss = pl.pallas_call(
            functools.partial(classify_kernel, "cols", n_cols),
            out_shape=(
                jax.ShapeDtypeStruct((classes, samples), jnp.bfloat16),
                jax.ShapeDtypeStruct((1, samples), jnp.float32),
            ),
            in_specs=[VM, VM],
            out_specs=(VM, VM),
            scratch_shapes=[
                pltpu.VMEM((n_cols, classes, samples), jnp.float32),
                pltpu.SemaphoreType.DMA((n_cols,)),
                pltpu.SemaphoreType.DMA((n_cols,)),
            ],
            compiler_params=pltpu.CompilerParams(collective_id=1, has_side_effects=True),
            name="classify",
        )(part, labels[step][None])
        losses.append(lax.dynamic_slice_in_dim(loss[0], lax.axis_index("cols") * owned, owned))
        grads = trade(
            slot_call(
                grads_kernel, step, tiles, scalars, residual, packed,
                [pltpu.VMEM((entries, classes, size), jnp.float32)], "grads",
            )
        )
        rate = lax.slice_in_dim(learning_rate, step, step + 1)
        shape = jax.ShapeDtypeStruct(current.shape, current.dtype)
        if step + 1 < steps:
            current, send = pl.pallas_call(
                functools.partial(apply_pack_kernel, size),
                out_shape=(shape, packed), in_specs=[SM, SM, SM, VM, VM], out_specs=(VM, VM),
                compiler_params=LOCAL, name="apply_pack",
            )(requests[step], requests[step + 1], rate, current, grads)
        else:
            current = pl.pallas_call(
                functools.partial(apply_kernel, size),
                out_shape=shape, in_specs=[SM, SM, VM, VM], out_specs=VM,
                compiler_params=LOCAL, name="apply",
            )(requests[step], rate, current, grads)
    return current, jnp.stack(losses)


def per_device(
    tiles, tile_scales, tile_rows, tile_cols, tile_counts, labels, learning_rate, weights
):
    args = (tiles, tile_scales, tile_rows, tile_cols, tile_counts, labels, learning_rate, weights)
    size, slots = tiles.shape[-1], tiles.shape[3]
    n_rows, n_cols = lax.axis_size("rows"), lax.axis_size("cols")
    per_owner = weights.shape[1] // size
    mean = slots / n_rows
    capacity = min(per_owner, slots, 4 * math.ceil((mean + 3 * math.sqrt(mean)) / 4))
    slot_ids = jnp.arange(slots, dtype=jnp.int32)

    live = slot_ids < tile_counts[:, 0, 0, None]
    mine = jnp.where(live, tile_cols[:, 0, 0], -1)
    everyone = lax.all_gather(mine, ("rows", "cols"), axis=0)
    owner = jnp.where(everyone >= 0, everyone // per_owner, -1)
    same = everyone[..., :, None] == everyone[..., None, :]
    before = slot_ids[:, None] > slot_ids[None, :]
    fresh = (everyone >= 0) & ~jnp.any(same & before, axis=-1)
    lower = (owner[..., :, None] == owner[..., None, :]) & (
        everyone[..., None, :] < everyone[..., :, None]
    )
    rank = jnp.sum((lower & fresh[..., None, :]).astype(jnp.int32), axis=-1)
    rank = jnp.where(everyone >= 0, rank, 0)
    most = jnp.max(rank) + 1

    row, col = lax.axis_index("rows"), lax.axis_index("cols")
    entry = jnp.where(everyone >= 0, owner * capacity + rank, 0)
    places = lax.dynamic_index_in_dim(entry, row * n_cols + col, 0, keepdims=False)
    places = jnp.minimum(places, n_rows * capacity - 1)
    group = lambda x: lax.dynamic_index_in_dim(
        x.reshape(n_rows, n_cols, *x.shape[1:]), col, 1, keepdims=False
    )
    picks = (
        (group(owner) == row)[..., None, :]
        & group(fresh)[..., None, :]
        & (group(rank)[..., None, :] == jnp.arange(capacity, dtype=jnp.int32)[:, None])
    )
    wanted = jnp.sum(
        jnp.where(picks, (group(everyone) - row * per_owner)[..., None, :], 0), axis=-1
    )
    requests = jnp.swapaxes(wanted, 0, 1).reshape(-1, n_rows * capacity)

    sparse = functools.partial(sparse_program, capacity)
    if capacity >= min(per_owner, slots):
        return sparse(places, requests, *args)
    return lax.cond(
        most <= capacity,
        sparse,
        lambda places, requests, *rest: dense_program(*rest),
        places, requests, *args,
    )


def solution(mesh):
    return jax.shard_map(
        per_device,
        mesh=mesh,
        in_specs=(
            P(None, "rows", "cols", None, None, None),
            P(None, "rows", "cols", None),
            P(None, "rows", "cols", None),
            P(None, "rows", "cols", None),
            P(None, "rows", "cols"),
            P(None, "rows"),
            P(),
            P(None, ("cols", "rows")),
        ),
        out_specs=(P(None, ("cols", "rows")), P(None, ("rows", "cols"))),
        check_vma=False,
    )
```

```python
import functools
import math
import jax
import jax.numpy as jnp
from jax import lax
from jax.experimental import pallas as pl
from jax.experimental.pallas import tpu as pltpu
from jax.sharding import PartitionSpec as P

MESH = pl.DeviceIdType.MESH
VMEM_LIMIT = 48 * 1024 * 1024
VM = pl.BlockSpec(memory_space=pltpu.VMEM)
SM = pl.BlockSpec(memory_space=pltpu.SMEM)
LOCAL = pltpu.CompilerParams(vmem_limit_bytes=VMEM_LIMIT)


def lanes(block, size):
    return pl.ds(pl.multiple_of(block * size, size), size)


def pack_body(size, next_ref, weights_ref, send_ref):
    @pl.loop(0, send_ref.shape[0] // 8)
    def _(group):
        for lane in range(8):
            entry = group * 8 + lane
            send_ref[entry] = weights_ref[:, lanes(next_ref[entry], size)].astype(jnp.bfloat16)


def apply_body(size, here_ref, rate_ref, weights_ref, grads_ref, out_ref):
    out_ref[...] = weights_ref[...]
    rate = rate_ref[0]

    @pl.loop(0, grads_ref.shape[0] // 8)
    def _(group):
        for lane in range(8):
            entry = group * 8 + lane
            where = lanes(here_ref[entry], size)
            out_ref[:, where] -= rate * grads_ref[entry].astype(jnp.float32)


def pack_kernel(size, next_ref, weights_ref, send_ref):
    pack_body(size, next_ref, weights_ref, send_ref)


def apply_kernel(size, here_ref, rate_ref, weights_ref, grads_ref, out_ref):
    apply_body(size, here_ref, rate_ref, weights_ref, grads_ref, out_ref)


def apply_pack_kernel(
    size, here_ref, next_ref, rate_ref, weights_ref, grads_ref, out_ref, send_ref
):
    apply_body(size, here_ref, rate_ref, weights_ref, grads_ref, out_ref)
    pack_body(size, next_ref, out_ref, send_ref)


def exchange_kernel(axis, count, send_ref, recv_ref, send_sems, recv_sems, own_sem):
    me = lax.axis_index(axis)
    barrier = pltpu.get_barrier_semaphore()
    for shift in range(1, count):
        peer = lax.rem(me + shift, count)
        pl.semaphore_signal(barrier, inc=1, device_id={axis: peer}, device_id_type=MESH)
    own = pltpu.make_async_copy(send_ref.at[me], recv_ref.at[me], own_sem)
    own.start()
    pl.semaphore_wait(barrier, count - 1)
    copies = []
    for shift in range(1, count):
        peer = lax.rem(me + shift, count)
        copy = pltpu.make_async_remote_copy(
            src_ref=send_ref.at[peer],
            dst_ref=recv_ref.at[me],
            send_sem=send_sems.at[shift],
            recv_sem=recv_sems.at[shift],
            device_id={axis: peer},
            device_id_type=MESH,
        )
        copy.start()
        copies.append(copy)
    own.wait()
    for copy in copies:
        copy.wait()


def exchange(send, axis, count, collective_id):
    return pl.pallas_call(
        functools.partial(exchange_kernel, axis, count),
        out_shape=jax.ShapeDtypeStruct(send.shape, send.dtype),
        in_specs=[VM],
        out_specs=VM,
        scratch_shapes=[
            pltpu.SemaphoreType.DMA((count,)),
            pltpu.SemaphoreType.DMA((count,)),
            pltpu.SemaphoreType.DMA,
        ],
        compiler_params=pltpu.CompilerParams(
            collective_id=collective_id, has_side_effects=True, vmem_limit_bytes=VMEM_LIMIT
        ),
        name="exchange",
    )(send)


def collect_kernel(n_rows, n_cols, mine_ref, all_ref, send_sems, recv_sems, own_sem):
    row, col = lax.axis_index("rows"), lax.axis_index("cols")
    row_peers = [lax.rem(row + shift, n_rows) for shift in range(1, n_rows)]
    col_peers = [lax.rem(col + shift, n_cols) for shift in range(1, n_cols)]
    barrier = pltpu.get_barrier_semaphore()
    for peer in row_peers:
        pl.semaphore_signal(barrier, inc=1, device_id={"rows": peer}, device_id_type=MESH)
    for peer in col_peers:
        pl.semaphore_signal(barrier, inc=1, device_id={"cols": peer}, device_id_type=MESH)
    own = pltpu.make_async_copy(mine_ref, all_ref.at[col, row], own_sem)
    own.start()
    pl.semaphore_wait(barrier, n_rows + n_cols - 2)
    copies = []
    for index, peer in enumerate(row_peers):
        copies.append(
            pltpu.make_async_remote_copy(
                src_ref=mine_ref,
                dst_ref=all_ref.at[col, row],
                send_sem=send_sems.at[index],
                recv_sem=recv_sems.at[index],
                device_id={"rows": peer},
                device_id_type=MESH,
            )
        )
        copies[-1].start()
    own.wait()
    for copy in copies:
        copy.wait()
    copies = []
    for index, peer in enumerate(col_peers):
        copies.append(
            pltpu.make_async_remote_copy(
                src_ref=all_ref.at[col],
                dst_ref=all_ref.at[col],
                send_sem=send_sems.at[n_rows + index],
                recv_sem=recv_sems.at[n_rows + index],
                device_id={"cols": peer},
                device_id_type=MESH,
            )
        )
        copies[-1].start()
    for copy in copies:
        copy.wait()


def collect(mine, n_rows, n_cols):
    return pl.pallas_call(
        functools.partial(collect_kernel, n_rows, n_cols),
        out_shape=jax.ShapeDtypeStruct((n_cols, n_rows, *mine.shape), mine.dtype),
        in_specs=[VM],
        out_specs=VM,
        scratch_shapes=[
            pltpu.SemaphoreType.DMA((n_rows + n_cols,)),
            pltpu.SemaphoreType.DMA((n_rows + n_cols,)),
            pltpu.SemaphoreType.DMA,
        ],
        compiler_params=pltpu.CompilerParams(collective_id=0, has_side_effects=True),
        name="collect",
    )(mine)


def scores_kernel(group, size, place_ref, row_ref, factor_ref, recv_ref, tiles_ref, out_ref):
    first = pl.program_id(0) * group

    @pl.when(first == 0)
    def _():
        out_ref[...] = jnp.zeros_like(out_ref)

    products = []
    for slot in range(group):
        product = lax.dot_general(
            recv_ref[place_ref[first + slot]],
            tiles_ref[0, 0, 0, slot],
            (((1,), (1,)), ((), ())),
            preferred_element_type=jnp.float32,
        )
        products.append(product * factor_ref[first + slot])
    for slot in range(group):
        out_ref[:, lanes(row_ref[first + slot], size)] += products[slot]


def classify_kernel(
    axis, count, part_ref, labels_ref, residual_ref, loss_ref, held, send_sems, recv_sems
):
    me = lax.axis_index(axis)
    barrier = pltpu.get_barrier_semaphore()
    for shift in range(1, count):
        peer = lax.rem(me + shift, count)
        pl.semaphore_signal(barrier, inc=1, device_id={axis: peer}, device_id_type=MESH)
    pl.semaphore_wait(barrier, count - 1)
    copies = []
    for shift in range(1, count):
        peer = lax.rem(me + shift, count)
        copy = pltpu.make_async_remote_copy(
            src_ref=part_ref,
            dst_ref=held.at[shift],
            send_sem=send_sems.at[shift],
            recv_sem=recv_sems.at[shift],
            device_id={axis: peer},
            device_id_type=MESH,
        )
        copy.start()
        copies.append(copy)
    scores = part_ref[...]
    for shift, copy in enumerate(copies):
        copy.wait()
        scores = scores + held[shift + 1]
    exp_scores = jnp.exp(scores)
    total = jnp.sum(exp_scores, axis=0, keepdims=True)
    class_ids = lax.broadcasted_iota(jnp.int32, scores.shape, 0)
    onehot = (class_ids == labels_ref[...]).astype(jnp.float32)
    loss_ref[...] = jnp.log(total) - jnp.sum(onehot * scores, axis=0, keepdims=True)
    residual_ref[...] = (exp_scores / total - onehot).astype(jnp.bfloat16)


def grads_kernel(
    group, size, place_ref, row_ref, factor_ref, residual_ref, tiles_ref, out_ref, total
):
    first = pl.program_id(0) * group

    @pl.when(first == 0)
    def _():
        total[...] = jnp.zeros_like(total)

    products = []
    for slot in range(group):
        product = jnp.dot(
            residual_ref[:, lanes(row_ref[first + slot], size)],
            tiles_ref[0, 0, 0, slot],
            preferred_element_type=jnp.float32,
        )
        products.append(product * factor_ref[first + slot])
    for slot in range(group):
        total[place_ref[first + slot]] += products[slot]

    @pl.when(pl.program_id(0) == pl.num_programs(0) - 1)
    def _():
        out_ref[...] = total[...].astype(jnp.bfloat16)


def slot_call(kernel, step, tiles, scalars, operand, out_shape, scratch, name):
    group = 16
    size = tiles.shape[-1]
    zeros = lambda rank: (lambda i, *_: (0,) * rank)
    return pl.pallas_call(
        functools.partial(kernel, group, size),
        grid_spec=pltpu.PrefetchScalarGridSpec(
            num_scalar_prefetch=3,
            grid=(tiles.shape[3] // group,),
            in_specs=[
                pl.BlockSpec(operand.shape, zeros(operand.ndim)),
                pl.BlockSpec((1, 1, 1, group, size, size), lambda i, *_: (step, 0, 0, i, 0, 0)),
            ],
            out_specs=pl.BlockSpec(out_shape.shape, zeros(len(out_shape.shape))),
            scratch_shapes=scratch,
        ),
        out_shape=out_shape,
        compiler_params=LOCAL,
        name=name,
    )(*scalars, operand, tiles)


def sparse_program(
    capacity, branch, owner, rank, requests,
    tiles, tile_scales, tile_rows, tile_cols, tile_counts, labels, learning_rate, weights
):
    classes = weights.shape[0]
    size = tiles.shape[-1]
    steps, slots = tiles.shape[0], tiles.shape[3]
    n_rows, n_cols = lax.axis_size("rows"), lax.axis_size("cols")
    samples = labels.shape[1]
    entries = n_rows * capacity
    packed = jax.ShapeDtypeStruct((entries, classes, size), jnp.bfloat16)
    slot_ids = jnp.arange(slots, dtype=jnp.int32)
    owned = samples // n_cols
    trade = lambda x: exchange(
        x.reshape(n_rows, capacity, classes, size), "rows", n_rows, 2 + branch
    ).reshape(packed.shape)

    places = owner * capacity + rank
    current = weights
    send = pl.pallas_call(
        functools.partial(pack_kernel, size),
        out_shape=packed, in_specs=[SM, VM], out_specs=VM, compiler_params=LOCAL, name="pack",
    )(requests[0], current)
    losses = []
    for step in range(steps):
        factor = jnp.where(slot_ids < tile_counts[step, 0, 0], tile_scales[step, 0, 0], 0.0)
        scalars = (places[step], tile_rows[step, 0, 0], factor)
        part = slot_call(
            scores_kernel, step, tiles, scalars, trade(send),
            jax.ShapeDtypeStruct((classes, samples), jnp.float32), [], "scores",
        )
        residual, loss = pl.pallas_call(
            functools.partial(classify_kernel, "cols", n_cols),
            out_shape=(
                jax.ShapeDtypeStruct((classes, samples), jnp.bfloat16),
                jax.ShapeDtypeStruct((1, samples), jnp.float32),
            ),
            in_specs=[VM, VM],
            out_specs=(VM, VM),
            scratch_shapes=[
                pltpu.VMEM((n_cols, classes, samples), jnp.float32),
                pltpu.SemaphoreType.DMA((n_cols,)),
                pltpu.SemaphoreType.DMA((n_cols,)),
            ],
            compiler_params=pltpu.CompilerParams(collective_id=1, has_side_effects=True),
            name="classify",
        )(part, labels[step][None])
        losses.append(lax.dynamic_slice_in_dim(loss[0], lax.axis_index("cols") * owned, owned))
        grads = trade(
            slot_call(
                grads_kernel, step, tiles, scalars, residual, packed,
                [pltpu.VMEM((entries, classes, size), jnp.float32)], "grads",
            )
        )
        rate = lax.slice_in_dim(learning_rate, step, step + 1)
        shape = jax.ShapeDtypeStruct(current.shape, current.dtype)
        if step + 1 < steps:
            current, send = pl.pallas_call(
                functools.partial(apply_pack_kernel, size),
                out_shape=(shape, packed), in_specs=[SM, SM, SM, VM, VM], out_specs=(VM, VM),
                compiler_params=LOCAL, name="apply_pack",
            )(requests[step], requests[step + 1], rate, current, grads)
        else:
            current = pl.pallas_call(
                functools.partial(apply_kernel, size),
                out_shape=shape, in_specs=[SM, SM, VM, VM], out_specs=VM,
                compiler_params=LOCAL, name="apply",
            )(requests[step], rate, current, grads)
    return current, jnp.stack(losses)


def per_device(
    tiles, tile_scales, tile_rows, tile_cols, tile_counts, labels, learning_rate, weights
):
    args = (tiles, tile_scales, tile_rows, tile_cols, tile_counts, labels, learning_rate, weights)
    size, slots = tiles.shape[-1], tiles.shape[3]
    n_rows, n_cols = lax.axis_size("rows"), lax.axis_size("cols")
    per_owner = weights.shape[1] // size
    full = min(per_owner, slots)
    mean = slots / n_rows
    tiers = [math.ceil(mean + spread * math.sqrt(mean)) for spread in (2, 2.5, 3, 4)]
    tiers = sorted({min(tier, full) for tier in tiers} | {full})
    slot_ids = jnp.arange(slots, dtype=jnp.int32)

    live = slot_ids < tile_counts[:, 0, 0, None]
    mine = jnp.where(live, tile_cols[:, 0, 0], -1)
    everyone = collect(mine, n_rows, n_cols)
    is_live = everyone >= 0
    owner = jnp.where(is_live, everyone // per_owner, -1)
    same = everyone[..., :, None] == everyone[..., None, :]
    before = slot_ids[:, None] > slot_ids[None, :]
    fresh = is_live & ~jnp.any(same & before, axis=-1)
    lower = (owner[..., :, None] == owner[..., None, :]) & (
        everyone[..., None, :] < everyone[..., :, None]
    )
    rank = jnp.sum((lower & fresh[..., None, :]).astype(jnp.int32), axis=-1)
    rank = jnp.where(is_live, rank, 0)
    most = jnp.max(rank) + 1

    row, col = lax.axis_index("rows"), lax.axis_index("cols")
    group = lambda x: lax.dynamic_index_in_dim(x, col, 0, keepdims=False)
    own = lambda x: lax.dynamic_index_in_dim(group(x), row, 0, keepdims=False)
    picks = (
        (group(owner) == row)[..., None, :]
        & group(fresh)[..., None, :]
        & (group(rank)[..., None, :] == jnp.arange(full, dtype=jnp.int32)[:, None])
    )
    wanted = jnp.sum(
        jnp.where(picks, (group(everyone) - row * per_owner)[..., None, :], 0), axis=-1
    )
    requests = jnp.swapaxes(wanted, 0, 1)

    def at_capacity(capacity, branch):
        def run(owner, rank, requests, *args):
            cut = requests[:, :, :capacity].reshape(requests.shape[0], -1)
            return sparse_program(capacity, branch, owner, rank, cut, *args)

        return run

    branches = [at_capacity(capacity, branch) for branch, capacity in enumerate(tiers)]
    operands = (jnp.maximum(own(owner), 0), own(rank), requests, *args)
    if len(branches) == 1:
        return branches[0](*operands)
    chosen = sum((most > tier).astype(jnp.int32) for tier in tiers[:-1])
    return lax.switch(chosen, branches, *operands)


def solution(mesh):
    return jax.shard_map(
        per_device,
        mesh=mesh,
        in_specs=(
            P(None, "rows", "cols", None, None, None),
            P(None, "rows", "cols", None),
            P(None, "rows", "cols", None),
            P(None, "rows", "cols", None),
            P(None, "rows", "cols"),
            P(None, "rows"),
            P(),
            P(None, ("cols", "rows")),
        ),
        out_specs=(P(None, ("cols", "rows")), P(None, ("rows", "cols"))),
        check_vma=False,
    )
```

```python
import functools
import math
import jax
import jax.numpy as jnp
from jax import lax
from jax.experimental import pallas as pl
from jax.experimental.pallas import tpu as pltpu
from jax.sharding import PartitionSpec as P

MESH = pl.DeviceIdType.MESH
VMEM_LIMIT = 48 * 1024 * 1024
VM = pl.BlockSpec(memory_space=pltpu.VMEM)
SM = pl.BlockSpec(memory_space=pltpu.SMEM)
LOCAL = pltpu.CompilerParams(vmem_limit_bytes=VMEM_LIMIT)
SLOTS = pltpu.CompilerParams(vmem_limit_bytes=48 * 1024 * 1024)


def lanes(block, size):
    return pl.ds(pl.multiple_of(block * size, size), size)


def pack_body(size, step, capacity, requests_ref, weights_ref, send_ref):
    owners = send_ref.shape[0] // capacity
    full = requests_ref.shape[1] // owners

    @pl.loop(0, capacity)
    def _(index):
        for peer in range(owners):
            where = lanes(requests_ref[step, peer * full + index], size)
            send_ref[peer * capacity + index] = weights_ref[:, where].astype(jnp.bfloat16)


def apply_body(size, step, capacity, requests_ref, rate_ref, weights_ref, grads_ref, out_ref):
    owners = grads_ref.shape[0] // capacity
    full = requests_ref.shape[1] // owners
    out_ref[...] = weights_ref[...]
    rate = rate_ref[step]

    @pl.loop(0, capacity)
    def _(index):
        for peer in range(owners):
            where = lanes(requests_ref[step, peer * full + index], size)
            grad = grads_ref[peer * capacity + index].astype(jnp.float32)
            out_ref[:, where] -= rate * grad


def apply_kernel(size, step, capacity, requests_ref, rate_ref, weights_ref, grads_ref, out_ref):
    apply_body(size, step, capacity, requests_ref, rate_ref, weights_ref, grads_ref, out_ref)


def apply_pack_kernel(
    size, step, capacity, requests_ref, rate_ref, weights_ref, grads_ref, out_ref, send_ref
):
    apply_body(size, step, capacity, requests_ref, rate_ref, weights_ref, grads_ref, out_ref)
    pack_body(size, step + 1, capacity, requests_ref, out_ref, send_ref)


def exchange_kernel(axis, count, send_ref, recv_ref, send_sems, recv_sems, own_sem):
    me = lax.axis_index(axis)
    barrier = pltpu.get_barrier_semaphore()
    for shift in range(1, count):
        peer = lax.rem(me + shift, count)
        pl.semaphore_signal(barrier, inc=1, device_id={axis: peer}, device_id_type=MESH)
    own = pltpu.make_async_copy(send_ref.at[me], recv_ref.at[me], own_sem)
    own.start()
    pl.semaphore_wait(barrier, count - 1)
    copies = []
    for shift in range(1, count):
        peer = lax.rem(me + shift, count)
        copy = pltpu.make_async_remote_copy(
            src_ref=send_ref.at[peer],
            dst_ref=recv_ref.at[me],
            send_sem=send_sems.at[shift],
            recv_sem=recv_sems.at[shift],
            device_id={axis: peer},
            device_id_type=MESH,
        )
        copy.start()
        copies.append(copy)
    own.wait()
    for copy in copies:
        copy.wait()


def exchange(send, axis, count, collective_id):
    return pl.pallas_call(
        functools.partial(exchange_kernel, axis, count),
        out_shape=jax.ShapeDtypeStruct(send.shape, send.dtype),
        in_specs=[VM],
        out_specs=VM,
        scratch_shapes=[
            pltpu.SemaphoreType.DMA((count,)),
            pltpu.SemaphoreType.DMA((count,)),
            pltpu.SemaphoreType.DMA,
        ],
        compiler_params=pltpu.CompilerParams(
            collective_id=collective_id, has_side_effects=True, vmem_limit_bytes=VMEM_LIMIT
        ),
        name="exchange",
    )(send)


def collect_kernel(n_rows, n_cols, mine_ref, all_ref, send_sems, recv_sems, own_sem):
    row, col = lax.axis_index("rows"), lax.axis_index("cols")
    row_peers = [lax.rem(row + shift, n_rows) for shift in range(1, n_rows)]
    col_peers = [lax.rem(col + shift, n_cols) for shift in range(1, n_cols)]
    barrier = pltpu.get_barrier_semaphore()
    for peer in row_peers:
        pl.semaphore_signal(barrier, inc=1, device_id={"rows": peer}, device_id_type=MESH)
    for peer in col_peers:
        pl.semaphore_signal(barrier, inc=1, device_id={"cols": peer}, device_id_type=MESH)
    own = pltpu.make_async_copy(mine_ref, all_ref.at[col, row], own_sem)
    own.start()
    pl.semaphore_wait(barrier, n_rows + n_cols - 2)
    copies = []
    for index, peer in enumerate(row_peers):
        copies.append(
            pltpu.make_async_remote_copy(
                src_ref=mine_ref,
                dst_ref=all_ref.at[col, row],
                send_sem=send_sems.at[index],
                recv_sem=recv_sems.at[index],
                device_id={"rows": peer},
                device_id_type=MESH,
            )
        )
        copies[-1].start()
    own.wait()
    for copy in copies:
        copy.wait()
    copies = []
    for index, peer in enumerate(col_peers):
        copies.append(
            pltpu.make_async_remote_copy(
                src_ref=all_ref.at[col],
                dst_ref=all_ref.at[col],
                send_sem=send_sems.at[n_rows + index],
                recv_sem=recv_sems.at[n_rows + index],
                device_id={"cols": peer},
                device_id_type=MESH,
            )
        )
        copies[-1].start()
    for copy in copies:
        copy.wait()


def collect(mine, n_rows, n_cols):
    return pl.pallas_call(
        functools.partial(collect_kernel, n_rows, n_cols),
        out_shape=jax.ShapeDtypeStruct((n_cols, n_rows, *mine.shape), mine.dtype),
        in_specs=[VM],
        out_specs=VM,
        scratch_shapes=[
            pltpu.SemaphoreType.DMA((n_rows + n_cols,)),
            pltpu.SemaphoreType.DMA((n_rows + n_cols,)),
            pltpu.SemaphoreType.DMA,
        ],
        compiler_params=pltpu.CompilerParams(collective_id=0, has_side_effects=True),
        name="collect",
    )(mine)


GROUP = 16


def slot_scalars(step, full, capacity, slot, code_ref, row_ref, scale_ref, count_ref):
    code = code_ref[step, slot]
    place = code // full * capacity + lax.rem(code, full)
    factor = jnp.where(slot < count_ref[step, 0, 0], scale_ref[step, 0, 0, slot], 0.0)
    return place, row_ref[step, 0, 0, slot], factor


def fetch_tiles(step, tiles_ref, held_ref, sems):
    def copy(group):
        part = pl.ds(group * GROUP, GROUP)
        return pltpu.make_async_copy(
            tiles_ref.at[step, 0, 0, part], held_ref.at[part], sems.at[group]
        )

    for group in range(held_ref.shape[0] // GROUP):
        copy(group).start()
    return lambda group: copy(group).wait()


def scores_kernel(
    step, full, capacity, code_ref, row_ref, scale_ref, count_ref, recv_ref, tiles_ref, out_ref,
    held_ref, sems,
):
    size = held_ref.shape[-1]
    arrived = fetch_tiles(step, tiles_ref, held_ref, sems)
    out_ref[...] = jnp.zeros_like(out_ref)

    @pl.loop(0, held_ref.shape[0] // GROUP)
    def _(group):
        arrived(group)
        products = []
        for lane in range(GROUP):
            slot = group * GROUP + lane
            place, row, factor = slot_scalars(
                step, full, capacity, slot, code_ref, row_ref, scale_ref, count_ref
            )
            product = lax.dot_general(
                recv_ref[place],
                held_ref[slot],
                (((1,), (1,)), ((), ())),
                preferred_element_type=jnp.float32,
            )
            products.append((row, product * factor))
        for row, product in products:
            out_ref[:, lanes(row, size)] += product


def classify_kernel(
    axis, count, step, part_ref, labels_ref, residual_ref, loss_ref, held, losses, send_sems,
    recv_sems,
):
    me = lax.axis_index(axis)
    barrier = pltpu.get_barrier_semaphore()
    for shift in range(1, count):
        peer = lax.rem(me + shift, count)
        pl.semaphore_signal(barrier, inc=1, device_id={axis: peer}, device_id_type=MESH)
    pl.semaphore_wait(barrier, count - 1)
    copies = []
    for shift in range(1, count):
        peer = lax.rem(me + shift, count)
        copy = pltpu.make_async_remote_copy(
            src_ref=part_ref,
            dst_ref=held.at[shift],
            send_sem=send_sems.at[shift],
            recv_sem=recv_sems.at[shift],
            device_id={axis: peer},
            device_id_type=MESH,
        )
        copy.start()
        copies.append(copy)
    scores = part_ref[...]
    for shift, copy in enumerate(copies):
        copy.wait()
        scores = scores + held[shift + 1]
    exp_scores = jnp.exp(scores)
    total = jnp.sum(exp_scores, axis=0, keepdims=True)
    class_ids = lax.broadcasted_iota(jnp.int32, scores.shape, 0)
    onehot = (class_ids == labels_ref[step : step + 1, :]).astype(jnp.float32)
    losses[...] = jnp.log(total) - jnp.sum(onehot * scores, axis=0, keepdims=True)
    if loss_ref.shape == losses.shape:
        loss_ref[...] = losses[...]
    else:
        loss_ref[...] = losses[:, lanes(me, loss_ref.shape[1])]
    residual_ref[...] = (exp_scores / total - onehot).astype(jnp.bfloat16)


def grads_kernel(
    step, full, capacity, code_ref, row_ref, scale_ref, count_ref, residual_ref, tiles_ref,
    out_ref, total, held_ref, sems,
):
    size = held_ref.shape[-1]
    arrived = fetch_tiles(step, tiles_ref, held_ref, sems)
    total[...] = jnp.zeros_like(total)

    @pl.loop(0, held_ref.shape[0] // GROUP)
    def _(group):
        arrived(group)
        products = []
        for lane in range(GROUP):
            slot = group * GROUP + lane
            place, row, factor = slot_scalars(
                step, full, capacity, slot, code_ref, row_ref, scale_ref, count_ref
            )
            product = jnp.dot(
                residual_ref[:, lanes(row, size)],
                held_ref[slot],
                preferred_element_type=jnp.float32,
            )
            products.append((place, product * factor))
        for place, product in products:
            total[place] += product

    out_ref[...] = total[...].astype(jnp.bfloat16)


def sparse_program(
    capacity, branch, code, requests,
    tiles, tile_scales, tile_rows, tile_cols, tile_counts, labels, learning_rate, weights
):
    classes = weights.shape[0]
    size = tiles.shape[-1]
    steps = tiles.shape[0]
    n_rows, n_cols = lax.axis_size("rows"), lax.axis_size("cols")
    full = requests.shape[1] // n_rows
    samples = labels.shape[1]
    entries = n_rows * capacity
    packed = jax.ShapeDtypeStruct((entries, classes, size), jnp.bfloat16)
    owned = samples // n_cols
    scalars = (code, tile_rows, tile_scales, tile_counts)
    trade_id = 1 + steps + branch
    slots = tiles.shape[3]
    in_hbm = pl.BlockSpec(memory_space=pltpu.HBM)
    tile_room = [pltpu.VMEM(tiles.shape[3:], tiles.dtype), pltpu.SemaphoreType.DMA((slots // GROUP,))]

    def trade(x):
        blocks = x.reshape(n_rows, capacity, classes, size)
        return exchange(blocks, "rows", n_rows, trade_id).reshape(packed.shape)

    current = weights
    send = pl.pallas_call(
        functools.partial(pack_body, size, 0, capacity),
        out_shape=packed, in_specs=[SM, VM], out_specs=VM, compiler_params=LOCAL, name="pack",
    )(requests, current)
    losses = []
    for step in range(steps):
        got = trade(send)
        part = pl.pallas_call(
            functools.partial(scores_kernel, step, full, capacity),
            out_shape=jax.ShapeDtypeStruct((classes, samples), jnp.float32),
            in_specs=[SM] * 4 + [VM, in_hbm], out_specs=VM, compiler_params=SLOTS,
            scratch_shapes=tile_room, name="scores",
        )(*scalars, got, tiles)
        residual, loss = pl.pallas_call(
            functools.partial(classify_kernel, "cols", n_cols, step),
            out_shape=(
                jax.ShapeDtypeStruct((classes, samples), jnp.bfloat16),
                jax.ShapeDtypeStruct((1, owned if owned % 128 == 0 else samples), jnp.float32),
            ),
            in_specs=[VM, VM],
            out_specs=(VM, VM),
            scratch_shapes=[
                pltpu.VMEM((n_cols, classes, samples), jnp.float32),
                pltpu.VMEM((1, samples), jnp.float32),
                pltpu.SemaphoreType.DMA((n_cols,)),
                pltpu.SemaphoreType.DMA((n_cols,)),
            ],
            compiler_params=pltpu.CompilerParams(collective_id=1 + step, has_side_effects=True),
            name="classify",
        )(part, labels)
        if owned % 128 != 0:
            start = lax.axis_index("cols") * owned
            loss = lax.dynamic_slice_in_dim(loss, start, owned, axis=1)
        losses.append(loss)
        grads = pl.pallas_call(
            functools.partial(grads_kernel, step, full, capacity),
            out_shape=packed,
            in_specs=[SM] * 4 + [VM, in_hbm], out_specs=VM, compiler_params=SLOTS,
            scratch_shapes=[pltpu.VMEM((entries, classes, size), jnp.float32), *tile_room],
            name="grads",
        )(*scalars, residual, tiles)
        grads = trade(grads)
        shape = jax.ShapeDtypeStruct(current.shape, current.dtype)
        more = step + 1 < steps
        current, *send = pl.pallas_call(
            functools.partial(apply_pack_kernel if more else apply_kernel, size, step, capacity),
            out_shape=(shape, packed) if more else (shape,),
            in_specs=[SM, SM, VM, VM], out_specs=(VM, VM) if more else (VM,),
            compiler_params=LOCAL, name="apply",
        )(requests, learning_rate, current, grads)
        send = send[0] if more else None
    return current, jnp.concatenate(losses)


def per_device(
    tiles, tile_scales, tile_rows, tile_cols, tile_counts, labels, learning_rate, weights
):
    args = (tiles, tile_scales, tile_rows, tile_cols, tile_counts, labels, learning_rate, weights)
    size, slots = tiles.shape[-1], tiles.shape[3]
    n_rows, n_cols = lax.axis_size("rows"), lax.axis_size("cols")
    per_owner = weights.shape[1] // size
    full = min(per_owner, slots)
    mean = slots / n_rows
    tiers = [math.ceil(mean + spread * math.sqrt(mean)) for spread in (2, 2.5, 3, 4)]
    tiers = sorted({min(tier, full) for tier in tiers} | {full})
    slot_ids = jnp.arange(slots, dtype=jnp.int32)

    live = slot_ids < tile_counts[:, 0, 0, None]
    mine = jnp.where(live, tile_cols[:, 0, 0], -1)
    owner = jnp.where(live, mine // per_owner, -1)
    same = mine[:, :, None] == mine[:, None, :]
    before = slot_ids[:, None] > slot_ids[None, :]
    fresh = live & ~jnp.any(same & before, axis=-1)
    lower = (owner[:, :, None] == owner[:, None, :]) & (mine[:, None, :] < mine[:, :, None])
    rank = jnp.sum((lower & fresh[:, None, :]).astype(jnp.int32), axis=-1)
    code = jnp.where(live, owner * full + rank, 0)
    everyone = collect(jnp.where(fresh, mine * full + rank, -1), n_rows, n_cols)
    most = jnp.max(jnp.where(everyone >= 0, everyone % full, 0)) + 1

    row, col = lax.axis_index("rows"), lax.axis_index("cols")
    peers = lax.dynamic_index_in_dim(everyone, col, 0, keepdims=False)
    local = peers // full - row * per_owner
    asked = (peers >= 0) & (local >= 0) & (local < per_owner)
    order = jnp.where(asked, peers % full, -1)
    picks = order[..., None, :] == jnp.arange(full, dtype=jnp.int32)[:, None]
    wanted = jnp.sum(jnp.where(picks, local[..., None, :], 0), axis=-1)
    requests = jnp.swapaxes(wanted, 0, 1).reshape(-1, n_rows * full)

    def at_capacity(capacity, branch):
        return functools.partial(sparse_program, capacity, branch)

    branches = [at_capacity(capacity, branch) for branch, capacity in enumerate(tiers)]
    operands = (code, requests, *args)
    if len(branches) == 1:
        return branches[0](*operands)
    chosen = sum((most > tier).astype(jnp.int32) for tier in tiers[:-1])
    return lax.switch(chosen, branches, *operands)


def solution(mesh):
    return jax.shard_map(
        per_device,
        mesh=mesh,
        in_specs=(
            P(None, "rows", "cols", None, None, None),
            P(None, "rows", "cols", None),
            P(None, "rows", "cols", None),
            P(None, "rows", "cols", None),
            P(None, "rows", "cols"),
            P(None, "rows"),
            P(),
            P(None, ("cols", "rows")),
        ),
        out_specs=(P(None, ("cols", "rows")), P(None, ("rows", "cols"))),
        check_vma=False,
    )
```

```python
import functools
import math
import jax
import jax.numpy as jnp
from jax import lax
from jax.experimental import pallas as pl
from jax.experimental.pallas import tpu as pltpu
from jax.sharding import PartitionSpec as P

MESH = pl.DeviceIdType.MESH
VMEM_LIMIT = 48 * 1024 * 1024
VM = pl.BlockSpec(memory_space=pltpu.VMEM)
SM = pl.BlockSpec(memory_space=pltpu.SMEM)
LOCAL = pltpu.CompilerParams(vmem_limit_bytes=VMEM_LIMIT)
SLOTS = pltpu.CompilerParams(vmem_limit_bytes=48 * 1024 * 1024)


def lanes(block, size):
    return pl.ds(pl.multiple_of(block * size, size), size)


def pack_body(size, step, capacity, requests_ref, weights_ref, send_ref):
    owners = send_ref.shape[0] // capacity
    full = requests_ref.shape[1] // owners

    @pl.loop(0, capacity)
    def _(index):
        for peer in range(owners):
            where = lanes(requests_ref[step, peer * full + index], size)
            send_ref[peer * capacity + index] = weights_ref[:, where].astype(jnp.bfloat16)


def apply_body(size, step, capacity, requests_ref, rate_ref, weights_ref, grads_ref, out_ref):
    owners = grads_ref.shape[0] // capacity
    full = requests_ref.shape[1] // owners
    out_ref[...] = weights_ref[...]
    rate = rate_ref[step]

    @pl.loop(0, capacity)
    def _(index):
        for peer in range(owners):
            where = lanes(requests_ref[step, peer * full + index], size)
            grad = grads_ref[peer * capacity + index].astype(jnp.float32)
            out_ref[:, where] -= rate * grad


def apply_kernel(size, step, capacity, requests_ref, rate_ref, weights_ref, grads_ref, out_ref):
    apply_body(size, step, capacity, requests_ref, rate_ref, weights_ref, grads_ref, out_ref)


def apply_pack_kernel(
    size, step, capacity, requests_ref, rate_ref, weights_ref, grads_ref, out_ref, send_ref
):
    apply_body(size, step, capacity, requests_ref, rate_ref, weights_ref, grads_ref, out_ref)
    pack_body(size, step + 1, capacity, requests_ref, out_ref, send_ref)


def exchange_kernel(axis, count, send_ref, recv_ref, send_sems, recv_sems, own_sem):
    me = lax.axis_index(axis)
    barrier = pltpu.get_barrier_semaphore()
    for shift in range(1, count):
        peer = lax.rem(me + shift, count)
        pl.semaphore_signal(barrier, inc=1, device_id={axis: peer}, device_id_type=MESH)
    own = pltpu.make_async_copy(send_ref.at[me], recv_ref.at[me], own_sem)
    own.start()
    pl.semaphore_wait(barrier, count - 1)
    copies = []
    for shift in sorted(range(1, count), key=lambda shift: abs(2 * shift - count)):
        peer = lax.rem(me + shift, count)
        copy = pltpu.make_async_remote_copy(
            src_ref=send_ref.at[peer],
            dst_ref=recv_ref.at[me],
            send_sem=send_sems.at[shift],
            recv_sem=recv_sems.at[shift],
            device_id={axis: peer},
            device_id_type=MESH,
        )
        copy.start()
        copies.append(copy)
    own.wait()
    for copy in copies:
        copy.wait()


def exchange(send, axis, count, collective_id):
    return pl.pallas_call(
        functools.partial(exchange_kernel, axis, count),
        out_shape=jax.ShapeDtypeStruct(send.shape, send.dtype),
        in_specs=[VM],
        out_specs=VM,
        scratch_shapes=[
            pltpu.SemaphoreType.DMA((count,)),
            pltpu.SemaphoreType.DMA((count,)),
            pltpu.SemaphoreType.DMA,
        ],
        compiler_params=pltpu.CompilerParams(
            collective_id=collective_id, has_side_effects=True, vmem_limit_bytes=VMEM_LIMIT
        ),
        name="exchange",
    )(send)


def collect_kernel(n_rows, n_cols, mine_ref, all_ref, send_sems, recv_sems, own_sem):
    row, col = lax.axis_index("rows"), lax.axis_index("cols")
    row_peers = [lax.rem(row + shift, n_rows) for shift in range(1, n_rows)]
    col_peers = [lax.rem(col + shift, n_cols) for shift in range(1, n_cols)]
    barrier = pltpu.get_barrier_semaphore()
    for peer in row_peers:
        pl.semaphore_signal(barrier, inc=1, device_id={"rows": peer}, device_id_type=MESH)
    for peer in col_peers:
        pl.semaphore_signal(barrier, inc=1, device_id={"cols": peer}, device_id_type=MESH)
    own = pltpu.make_async_copy(mine_ref, all_ref.at[col, row], own_sem)
    own.start()
    pl.semaphore_wait(barrier, n_rows + n_cols - 2)
    copies = []
    for index, peer in enumerate(row_peers):
        copies.append(
            pltpu.make_async_remote_copy(
                src_ref=mine_ref,
                dst_ref=all_ref.at[col, row],
                send_sem=send_sems.at[index],
                recv_sem=recv_sems.at[index],
                device_id={"rows": peer},
                device_id_type=MESH,
            )
        )
        copies[-1].start()
    own.wait()
    for copy in copies:
        copy.wait()
    copies = []
    for index, peer in enumerate(col_peers):
        copies.append(
            pltpu.make_async_remote_copy(
                src_ref=all_ref.at[col],
                dst_ref=all_ref.at[col],
                send_sem=send_sems.at[n_rows + index],
                recv_sem=recv_sems.at[n_rows + index],
                device_id={"cols": peer},
                device_id_type=MESH,
            )
        )
        copies[-1].start()
    for copy in copies:
        copy.wait()


def collect(mine, n_rows, n_cols):
    return pl.pallas_call(
        functools.partial(collect_kernel, n_rows, n_cols),
        out_shape=jax.ShapeDtypeStruct((n_cols, n_rows, *mine.shape), mine.dtype),
        in_specs=[VM],
        out_specs=VM,
        scratch_shapes=[
            pltpu.SemaphoreType.DMA((n_rows + n_cols,)),
            pltpu.SemaphoreType.DMA((n_rows + n_cols,)),
            pltpu.SemaphoreType.DMA,
        ],
        compiler_params=pltpu.CompilerParams(collective_id=0, has_side_effects=True),
        name="collect",
    )(mine)


GROUP = 16


def slot_scalars(step, full, capacity, slot, code_ref, row_ref, scale_ref, count_ref):
    code = code_ref[step, slot]
    place = code // full * capacity + lax.rem(code, full)
    factor = jnp.where(slot < count_ref[step, 0, 0], scale_ref[step, 0, 0, slot], 0.0)
    return place, row_ref[step, 0, 0, slot], factor


def fetch_tiles(step, tiles_ref, held_ref, sems):
    def copy(group):
        part = pl.ds(group * GROUP, GROUP)
        return pltpu.make_async_copy(
            tiles_ref.at[step, 0, 0, part], held_ref.at[part], sems.at[group]
        )

    for group in range(held_ref.shape[0] // GROUP):
        copy(group).start()
    return lambda group: copy(group).wait()


def scores_kernel(
    step, full, capacity, code_ref, row_ref, scale_ref, count_ref, recv_ref, tiles_ref, out_ref,
    held_ref, sems,
):
    size = held_ref.shape[-1]
    arrived = fetch_tiles(step, tiles_ref, held_ref, sems)
    out_ref[...] = jnp.zeros_like(out_ref)

    @pl.loop(0, held_ref.shape[0] // GROUP)
    def _(group):
        arrived(group)
        products = []
        for lane in range(GROUP):
            slot = group * GROUP + lane
            place, row, factor = slot_scalars(
                step, full, capacity, slot, code_ref, row_ref, scale_ref, count_ref
            )
            product = lax.dot_general(
                recv_ref[place],
                held_ref[slot],
                (((1,), (1,)), ((), ())),
                preferred_element_type=jnp.float32,
            )
            products.append((row, product * factor))
        for row, product in products:
            out_ref[:, lanes(row, size)] += product


def classify_kernel(
    axis, count, step, part_ref, labels_ref, residual_ref, loss_ref, held, losses, send_sems,
    recv_sems,
):
    me = lax.axis_index(axis)
    barrier = pltpu.get_barrier_semaphore()
    for shift in range(1, count):
        peer = lax.rem(me + shift, count)
        pl.semaphore_signal(barrier, inc=1, device_id={axis: peer}, device_id_type=MESH)
    pl.semaphore_wait(barrier, count - 1)
    copies = []
    for shift in range(1, count):
        peer = lax.rem(me + shift, count)
        copy = pltpu.make_async_remote_copy(
            src_ref=part_ref,
            dst_ref=held.at[shift],
            send_sem=send_sems.at[shift],
            recv_sem=recv_sems.at[shift],
            device_id={axis: peer},
            device_id_type=MESH,
        )
        copy.start()
        copies.append(copy)
    scores = part_ref[...]
    for shift, copy in enumerate(copies):
        copy.wait()
        scores = scores + held[shift + 1]
    exp_scores = jnp.exp(scores)
    total = jnp.sum(exp_scores, axis=0, keepdims=True)
    class_ids = lax.broadcasted_iota(jnp.int32, scores.shape, 0)
    onehot = (class_ids == labels_ref[step : step + 1, :]).astype(jnp.float32)
    losses[...] = jnp.log(total) - jnp.sum(onehot * scores, axis=0, keepdims=True)
    if loss_ref.shape == losses.shape:
        loss_ref[...] = losses[...]
    else:
        loss_ref[...] = losses[:, lanes(me, loss_ref.shape[1])]
    residual_ref[...] = (exp_scores / total - onehot).astype(jnp.bfloat16)


def grads_kernel(
    step, full, capacity, code_ref, row_ref, scale_ref, count_ref, residual_ref, tiles_ref,
    out_ref, total, held_ref, sems,
):
    size = held_ref.shape[-1]
    arrived = fetch_tiles(step, tiles_ref, held_ref, sems)
    total[...] = jnp.zeros_like(total)

    @pl.loop(0, held_ref.shape[0] // GROUP)
    def _(group):
        arrived(group)
        products = []
        for lane in range(GROUP):
            slot = group * GROUP + lane
            place, row, factor = slot_scalars(
                step, full, capacity, slot, code_ref, row_ref, scale_ref, count_ref
            )
            product = jnp.dot(
                residual_ref[:, lanes(row, size)],
                held_ref[slot],
                preferred_element_type=jnp.float32,
            )
            products.append((place, product * factor))
        for place, product in products:
            total[place] += product

    out_ref[...] = total[...].astype(jnp.bfloat16)


def sparse_program(
    capacity, branch, code, requests,
    tiles, tile_scales, tile_rows, tile_cols, tile_counts, labels, learning_rate, weights
):
    classes = weights.shape[0]
    size = tiles.shape[-1]
    steps = tiles.shape[0]
    n_rows, n_cols = lax.axis_size("rows"), lax.axis_size("cols")
    full = requests.shape[1] // n_rows
    samples = labels.shape[1]
    entries = n_rows * capacity
    packed = jax.ShapeDtypeStruct((entries, classes, size), jnp.bfloat16)
    owned = samples // n_cols
    scalars = (code, tile_rows, tile_scales, tile_counts)
    trade_id = 1 + steps + branch
    slots = tiles.shape[3]
    in_hbm = pl.BlockSpec(memory_space=pltpu.HBM)
    tile_room = [pltpu.VMEM(tiles.shape[3:], tiles.dtype), pltpu.SemaphoreType.DMA((slots // GROUP,))]

    def trade(x):
        blocks = x.reshape(n_rows, capacity, classes, size)
        return exchange(blocks, "rows", n_rows, trade_id).reshape(packed.shape)

    current = weights
    send = pl.pallas_call(
        functools.partial(pack_body, size, 0, capacity),
        out_shape=packed, in_specs=[SM, VM], out_specs=VM, compiler_params=LOCAL, name="pack",
    )(requests, current)
    losses = []
    for step in range(steps):
        got = trade(send)
        part = pl.pallas_call(
            functools.partial(scores_kernel, step, full, capacity),
            out_shape=jax.ShapeDtypeStruct((classes, samples), jnp.float32),
            in_specs=[SM] * 4 + [VM, in_hbm], out_specs=VM, compiler_params=SLOTS,
            scratch_shapes=tile_room, name="scores",
        )(*scalars, got, tiles)
        residual, loss = pl.pallas_call(
            functools.partial(classify_kernel, "cols", n_cols, step),
            out_shape=(
                jax.ShapeDtypeStruct((classes, samples), jnp.bfloat16),
                jax.ShapeDtypeStruct((1, owned if owned % 128 == 0 else samples), jnp.float32),
            ),
            in_specs=[VM, VM],
            out_specs=(VM, VM),
            scratch_shapes=[
                pltpu.VMEM((n_cols, classes, samples), jnp.float32),
                pltpu.VMEM((1, samples), jnp.float32),
                pltpu.SemaphoreType.DMA((n_cols,)),
                pltpu.SemaphoreType.DMA((n_cols,)),
            ],
            compiler_params=pltpu.CompilerParams(collective_id=1 + step, has_side_effects=True),
            name="classify",
        )(part, labels)
        if owned % 128 != 0:
            start = lax.axis_index("cols") * owned
            loss = lax.dynamic_slice_in_dim(loss, start, owned, axis=1)
        losses.append(loss)
        grads = pl.pallas_call(
            functools.partial(grads_kernel, step, full, capacity),
            out_shape=packed,
            in_specs=[SM] * 4 + [VM, in_hbm], out_specs=VM, compiler_params=SLOTS,
            scratch_shapes=[pltpu.VMEM((entries, classes, size), jnp.float32), *tile_room],
            name="grads",
        )(*scalars, residual, tiles)
        grads = trade(grads)
        shape = jax.ShapeDtypeStruct(current.shape, current.dtype)
        more = step + 1 < steps
        current, *send = pl.pallas_call(
            functools.partial(apply_pack_kernel if more else apply_kernel, size, step, capacity),
            out_shape=(shape, packed) if more else (shape,),
            in_specs=[SM, SM, VM, VM], out_specs=(VM, VM) if more else (VM,),
            compiler_params=LOCAL, name="apply",
        )(requests, learning_rate, current, grads)
        send = send[0] if more else None
    return current, jnp.concatenate(losses)


def per_device(
    tiles, tile_scales, tile_rows, tile_cols, tile_counts, labels, learning_rate, weights
):
    args = (tiles, tile_scales, tile_rows, tile_cols, tile_counts, labels, learning_rate, weights)
    size, slots = tiles.shape[-1], tiles.shape[3]
    n_rows, n_cols = lax.axis_size("rows"), lax.axis_size("cols")
    per_owner = weights.shape[1] // size
    full = min(per_owner, slots)
    mean = slots / n_rows
    tiers = [math.ceil(mean + spread * math.sqrt(mean)) for spread in (1.75, 2, 2.25, 2.5, 3, 4)]
    tiers = sorted({min(tier, full) for tier in tiers} | {full})
    slot_ids = jnp.arange(slots, dtype=jnp.int32)

    live = slot_ids < tile_counts[:, 0, 0, None]
    mine = jnp.where(live, tile_cols[:, 0, 0], -1)
    owner = jnp.where(live, mine // per_owner, -1)
    same = mine[:, :, None] == mine[:, None, :]
    before = slot_ids[:, None] > slot_ids[None, :]
    fresh = live & ~jnp.any(same & before, axis=-1)
    lower = (owner[:, :, None] == owner[:, None, :]) & (mine[:, None, :] < mine[:, :, None])
    rank = jnp.sum((lower & fresh[:, None, :]).astype(jnp.int32), axis=-1)
    code = jnp.where(live, owner * full + rank, 0)
    everyone = collect(jnp.where(fresh, mine * full + rank, -1), n_rows, n_cols)
    most = jnp.max(jnp.where(everyone >= 0, everyone % full, 0)) + 1

    row, col = lax.axis_index("rows"), lax.axis_index("cols")
    peers = lax.dynamic_index_in_dim(everyone, col, 0, keepdims=False)
    local = peers // full - row * per_owner
    asked = (peers >= 0) & (local >= 0) & (local < per_owner)
    order = jnp.where(asked, peers % full, -1)
    picks = order[..., None, :] == jnp.arange(full, dtype=jnp.int32)[:, None]
    wanted = jnp.sum(jnp.where(picks, local[..., None, :], 0), axis=-1)
    requests = jnp.swapaxes(wanted, 0, 1).reshape(-1, n_rows * full)

    def at_capacity(capacity, branch):
        return functools.partial(sparse_program, capacity, branch)

    branches = [at_capacity(capacity, branch) for branch, capacity in enumerate(tiers)]
    operands = (code, requests, *args)
    if len(branches) == 1:
        return branches[0](*operands)
    chosen = sum((most > tier).astype(jnp.int32) for tier in tiers[:-1])
    return lax.switch(chosen, branches, *operands)


def solution(mesh):
    return jax.shard_map(
        per_device,
        mesh=mesh,
        in_specs=(
            P(None, "rows", "cols", None, None, None),
            P(None, "rows", "cols", None),
            P(None, "rows", "cols", None),
            P(None, "rows", "cols", None),
            P(None, "rows", "cols"),
            P(None, "rows"),
            P(),
            P(None, ("cols", "rows")),
        ),
        out_specs=(P(None, ("cols", "rows")), P(None, ("rows", "cols"))),
        check_vma=False,
    )
```
